32 devices in a mesh: sec: 2 (over core), var: 4 (over z), trait: 4 (over y, x).
Axes of the slice: x: 2, y: 2, z: 4, core: 2. Of those that a mesh axis runs over, the one named last changes fastest.
Arguments:
- z_typed: bfloat16 [32768, 512], P(('sec', 'var'), 'trait'), may hold values from -6 to 6
- band_inverse: bfloat16 [256, 128, 384], P(('sec', 'var')), may hold values from -0.3125 to 0.3125
- ld_untyped: bfloat16 [512, 128, 512], P(('sec', 'var')), may hold values from -0.375 to 0.375
- trait_mix: bfloat16 [512, 512], replicated, may hold values from -0.25 to 0.25
- win_start: int32 [512], P(('sec', 'var')), may hold values from 0 to 255, as said below
- win_count: int32 [512], P(('sec', 'var')), may hold values from 1 to 4, as said below
Outputs:
- imputed_mixed: bfloat16 [65536, 512], P(('sec', 'var'), 'trait')
The draws below stay inside these ranges and needn't reach their ends.
Inputs may be any that keep to these rules, and one draw needn't show every extreme that they name: Windows follow chromosome order: within the 64 untyped blocks of one index g of sec+var, win_start never falls, and every window lies in typed blocks g * 32 - 32 to (g + 1) * 32 + 31; the first window of each index starts at its lower end (or at 0) and the last one ends at its upper end (or at the chromosome's end). win_start + win_count never exceeds 256.
All inputs are finite; a program needn't handle non-finite values.
Results may differ from the reference program's by a relative error of at most 0.0057.
Values may be sent and summed in bfloat16 or wider, within the bound.
A program may use at most 64 MiB of HBM per device.

```python
import jax
import jax.numpy as jnp
from jax import lax

BLK = 128
WIN = 4
TRAITS = 512
TB_DEV = 32
UB_DEV = 64
REACH = 32
VGROUPS = 8
TYPED_BLOCKS = 256
TYPED_ROWS = 32768
UNTYPED_BLOCKS = 512


def window_plan(key):
    subkeys = jax.random.split(jax.random.fold_in(key, 7), VGROUPS)
    owners = jnp.arange(VGROUPS, dtype=jnp.int32)
    span = TB_DEV + 2 * REACH - WIN

    def one_owner(owner_key, owner):
        first_key, second_key = jax.random.split(owner_key, 2)
        lowest = owner * TB_DEV - REACH
        offsets = jnp.sort(jax.random.randint(first_key, (UB_DEV,), 0, span + 1))
        offsets = offsets.at[0].set(0).at[UB_DEV - 1].set(span)
        counts = jax.random.randint(second_key, (UB_DEV,), 1, WIN + 1)
        counts = counts.at[0].set(WIN).at[UB_DEV - 1].set(WIN)
        starts = jnp.clip(lowest + offsets, 0, TYPED_BLOCKS - 1)
        counts = jnp.minimum(counts, TYPED_BLOCKS - starts)
        return (starts, counts)
    starts, counts = jax.vmap(one_owner)(subkeys, owners)
    return (starts.reshape(-1).astype(jnp.int32), counts.reshape(-1).astype(jnp.int32))


def draw_win_start(key, part):
    return window_plan(key)[0]


def draw_win_count(key, part):
    return window_plan(key)[1]


def block_levels(own_key, extent, cuts, low, top_value):
    loudness = 1.0
    for axis_at, blocks in cuts:
        heights = jax.random.uniform(jax.random.fold_in(jax.random.fold_in(own_key, 6), axis_at), (blocks,), jnp.float32, low / len(cuts), top_value / len(cuts))
        loudness = loudness * jnp.repeat(jnp.exp(heights), extent[axis_at] // blocks).reshape((-1,) + (1,) * (len(extent) - 1 - axis_at))
    return loudness


def gaussian(key, shape, deviation, limit, shards=(), kind=jnp.bfloat16):
    values = jax.random.normal(key, shape, jnp.float32) * deviation
    if len(shards) > 0:
        values = block_levels(key, shape, shards, -0.22, 0.18) * values
    return jnp.clip(values, min=-limit, max=limit).astype(kind)


def setup_inputs(seed: int = 0) -> dict:
    streams_of = jax.random.split(jax.random.key(seed), 7)
    return {
        "z_typed": gaussian(streams_of[0], (TYPED_ROWS, TRAITS), 1.0, 6.0, ((0, 8), (1, 4))),
        "band_inverse": gaussian(streams_of[1], (TYPED_BLOCKS, BLK, 3 * BLK), (3 * BLK) ** -0.5, 0.3125, ((0, 8),)),
        "ld_untyped": gaussian(streams_of[2], (UNTYPED_BLOCKS, BLK, WIN * BLK), (2 * BLK) ** -0.5, 0.375, ((0, 8),)),
        "trait_mix": gaussian(streams_of[3], (TRAITS, TRAITS), TRAITS ** -0.5, 0.25),
        "win_start": draw_win_start(jax.random.fold_in(streams_of[6], 71), 0),
        "win_count": draw_win_count(jax.random.fold_in(streams_of[6], 71), 0),
    }


def whiten(z_typed, band_inverse):
    blocks = z_typed.shape[0] // BLK
    padded = jnp.pad(z_typed, ((BLK, BLK), (0, 0)))
    stacked = jnp.concatenate([padded[k * BLK:(k + blocks) * BLK].reshape(blocks, BLK, z_typed.shape[1]) for k in range(3)], axis=1)
    return jnp.einsum("bij,bjc->bic", band_inverse.astype(jnp.float32), stacked.astype(jnp.float32)).astype(jnp.bfloat16)


def reference(z_typed, band_inverse, ld_untyped, trait_mix, win_start, win_count):
    whitened = whiten(z_typed, band_inverse)
    mixed = jnp.dot(whitened.reshape(TYPED_ROWS, TRAITS), trait_mix, preferred_element_type=jnp.float32).astype(jnp.bfloat16)
    mixed = mixed.reshape(TYPED_BLOCKS, BLK, TRAITS)
    window_steps = jnp.arange(WIN, dtype=jnp.int32)

    def impute(inputs):
        ld_group, starts, counts = inputs
        wanted = (starts[:, None] + window_steps[None, :]).astype(jnp.int32)
        usable = window_steps[None, :] < counts[:, None]
        picked = mixed[jnp.clip(wanted, 0, TYPED_BLOCKS - 1)]
        picked = jnp.where(usable[:, :, None, None], picked, jnp.zeros_like(picked))
        picked = picked.reshape(picked.shape[0], WIN * BLK, TRAITS)
        return jnp.einsum("uij,ujc->uic", ld_group.astype(jnp.float32), picked.astype(jnp.float32)).astype(jnp.bfloat16)

    grouped = (ld_untyped.reshape(VGROUPS, UB_DEV, BLK, WIN * BLK), win_start.reshape(VGROUPS, UB_DEV), win_count.reshape(VGROUPS, UB_DEV))
    imputed = lax.map(impute, grouped)
    return imputed.reshape(UNTYPED_BLOCKS * BLK, TRAITS)
```

```python
import functools

import jax
import jax.numpy as jnp
from jax import lax
from jax.experimental import pallas as pl
from jax.experimental.pallas import tpu as pltpu
from jax.sharding import PartitionSpec as P

BLK = 128
WIN = 4
CHUNK_BLOCKS = 4
AHEAD = 2
UNTYPED_TILE = 8
MESH = pl.DeviceIdType.MESH


def mixed_kernel(
    chunks, blocks, groups, var_size,
    z_ref, band_ref, mix_ref, ext_ref,
    zb, bandv, w, mv, mx,
    z_sem, band_sem, mix_sem, own_sem, edge_send, edge_recv, xy_send, xy_recv, halo_send, halo_recv,
):
    t = lax.axis_index("trait")
    g = lax.axis_index("sec") * var_size + lax.axis_index("var")
    x_peer = t + 1 - 2 * lax.rem(t, 2)
    y_peer = t + 2 - 4 * (t // 2)
    far_peer = x_peer + y_peer - t
    x_dev, y_dev = {"trait": x_peer}, {"trait": y_peer}
    right = {"sec": (g + 1) // var_size, "var": lax.rem(g + 1, var_size)}
    left_g = lax.rem(g + groups - 1, groups)
    left = {"sec": left_g // var_size, "var": lax.rem(left_g, var_size)}
    has_left, has_right = g > 0, g < groups - 1
    rows = blocks * BLK
    chunk = CHUNK_BLOCKS * BLK
    half = chunk // 2

    barrier = pltpu.get_barrier_semaphore()

    def greet(device):
        pl.semaphore_signal(barrier, inc=1, device_id=device, device_id_type=MESH)

    greet(x_dev)
    greet(y_dev)
    pl.when(has_left)(lambda: greet(left))
    pl.when(has_right)(lambda: greet(right))

    def remote(src, dst, send, recv, device):
        return pltpu.make_async_remote_copy(
            src_ref=src, dst_ref=dst, send_sem=send, recv_sem=recv,
            device_id=device, device_id_type=MESH,
        )

    load_z = pltpu.make_async_copy(z_ref, zb.at[pl.ds(BLK, rows)], z_sem)
    load_z.start()
    order = [(i + 1) % chunks for i in range(chunks)]

    def load_band(c):
        part = pl.ds(c * CHUNK_BLOCKS, CHUNK_BLOCKS)
        return pltpu.make_async_copy(band_ref.at[part], bandv.at[part], band_sem.at[c])

    for c in order:
        load_band(c).start()
    columns = pl.ds(pl.multiple_of(t * BLK, BLK), BLK)
    load_mix = [
        pltpu.make_async_copy(
            mix_ref.at[pl.ds(pl.multiple_of(peer * BLK, BLK), BLK), columns],
            mv.at[pl.ds(j * BLK, BLK)],
            mix_sem.at[j],
        )
        for j, peer in enumerate((t, x_peer, y_peer, far_peer))
    ]
    for copy in load_mix:
        copy.start()

    @pl.when(jnp.logical_not(has_left))
    def _():
        zb[pl.ds(0, BLK), :] = jnp.zeros((BLK, BLK), zb.dtype)

    @pl.when(jnp.logical_not(has_right))
    def _():
        zb[pl.ds(rows + BLK, BLK), :] = jnp.zeros((BLK, BLK), zb.dtype)

    edge_right = remote(
        z_ref.at[pl.ds(rows - BLK, BLK)], zb.at[pl.ds(0, BLK)], edge_send.at[0], edge_recv.at[0], right
    )
    edge_left = remote(
        z_ref.at[pl.ds(0, BLK)], zb.at[pl.ds(rows + BLK, BLK)], edge_send.at[1], edge_recv.at[1], left
    )

    def whiten(c):
        load_band(c).wait()
        if c == chunks - 1:
            pl.when(has_right)(edge_left.wait_recv)
        if c == 0:
            pl.when(has_left)(edge_right.wait_recv)

        def one(i, carry):
            b = c * CHUNK_BLOCKS + i
            first = pl.multiple_of(b * BLK, BLK)
            sums = jnp.dot(bandv[b], zb[pl.ds(first, 3 * BLK), :], preferred_element_type=jnp.float32)
            w[0, pl.ds(first, BLK), :] = sums.astype(w.dtype)
            return carry

        lax.fori_loop(0, CHUNK_BLOCKS, one, 0)

    def own_sends(c):
        part = pl.ds(c * chunk, chunk)
        return (
            remote(w.at[0, part], w.at[1, part], xy_send.at[0, c], xy_recv.at[0, c], x_dev),
            remote(w.at[0, part], w.at[2, part], xy_send.at[1, c], xy_recv.at[1, c], y_dev),
        )

    def relays(c):
        lower, upper = pl.ds(c * chunk, half), pl.ds(c * chunk + half, half)
        return (
            remote(w.at[1, lower], w.at[3, lower], xy_send.at[2, c], xy_recv.at[2, c], y_dev),
            remote(w.at[2, upper], w.at[3, upper], xy_send.at[3, c], xy_recv.at[3, c], x_dev),
        )

    def halos(c):
        part = pl.ds(c * chunk, chunk)
        return (
            remote(mx.at[part], ext_ref.at[part], halo_send.at[0, c], halo_recv.at[0, c], right),
            remote(
                mx.at[part], ext_ref.at[pl.ds(2 * rows + c * chunk, chunk)],
                halo_send.at[1, c], halo_recv.at[1, c], left,
            ),
        )

    def keep(c):
        return pltpu.make_async_copy(
            mx.at[pl.ds(c * chunk, chunk)], ext_ref.at[pl.ds(rows + c * chunk, chunk)], own_sem.at[c]
        )

    def mix(c):
        part = pl.ds(c * chunk, chunk)
        all_traits = jnp.concatenate([w[j, part, :] for j in range(4)], axis=1)
        sums = jnp.dot(all_traits, mv[...], preferred_element_type=jnp.float32)
        mx[part, :] = sums.astype(mx.dtype)

    load_z.wait()
    for c in order[: AHEAD + 1]:
        whiten(c)
    pl.semaphore_wait(barrier, 2 + has_left.astype(jnp.int32) + has_right.astype(jnp.int32))
    pl.when(has_right)(edge_right.start)
    pl.when(has_left)(edge_left.start)
    for c in order[:AHEAD]:
        for copy in own_sends(c):
            copy.start()
    for copy in load_mix:
        copy.wait()
    for i in range(chunks + 1):
        if i < chunks:
            for copy in own_sends(order[i]):
                copy.wait_recv()
            for copy in relays(order[i]):
                copy.start()
            if i + AHEAD < chunks:
                for copy in own_sends(order[i + AHEAD]):
                    copy.start()
        if i >= 1:
            c = order[i - 1]
            for copy in relays(c):
                copy.wait_recv()
            mix(c)
            to_right, to_left = halos(c)
            pl.when(has_right)(to_right.start)
            pl.when(has_left)(to_left.start)
            keep(c).start()
        if i + AHEAD + 1 < chunks:
            whiten(order[i + AHEAD + 1])
    for c in order:
        for copy in own_sends(c) + relays(c):
            copy.wait_send()
        keep(c).wait()
        to_right, to_left = halos(c)

        @pl.when(has_right)
        def _():
            to_right.wait_send()
            to_left.wait_recv()

        @pl.when(has_left)
        def _():
            to_left.wait_send()
            to_right.wait_recv()

    pl.when(has_right)(edge_right.wait_send)
    pl.when(has_left)(edge_left.wait_send)


def mixed_with_neighbours(z_typed, band_inverse, trait_mix, groups, var_size):
    rows = z_typed.shape[0]
    blocks = rows // BLK
    chunks = blocks // CHUNK_BLOCKS
    dma = pltpu.SemaphoreType.DMA
    kind = z_typed.dtype
    return pl.pallas_call(
        functools.partial(mixed_kernel, chunks, blocks, groups, var_size),
        out_shape=jax.ShapeDtypeStruct((3 * rows, BLK), kind),
        in_specs=[pl.BlockSpec(memory_space=pl.ANY)] * 3,
        out_specs=pl.BlockSpec(memory_space=pl.ANY),
        scratch_shapes=[
            pltpu.VMEM((rows + 2 * BLK, BLK), kind),
            pltpu.VMEM(band_inverse.shape, kind),
            pltpu.VMEM((4, rows, BLK), kind),
            pltpu.VMEM((4 * BLK, BLK), kind),
            pltpu.VMEM((rows, BLK), kind),
            dma, dma((chunks,)), dma((4,)), dma((chunks,)),
            dma((2,)), dma((2,)),
            dma((4, chunks)), dma((4, chunks)),
            dma((2, chunks)), dma((2, chunks)),
        ],
        compiler_params=pltpu.CompilerParams(
            collective_id=0, has_side_effects=True, vmem_limit_bytes=16 * 1024 * 1024
        ),
        name="mixed_kernel",
    )(z_typed, band_inverse, trait_mix)


def impute_kernel(blocks, var_size, start_ref, count_ref, ext_ref, ld_ref, out_ref):
    g = lax.axis_index("sec") * var_size + lax.axis_index("var")
    tile = ld_ref.shape[0]
    first = pl.program_id(0) * tile
    for i in range(tile):
        start = start_ref[first + i] - (g - 1) * blocks
        count = count_ref[first + i]
        parts = []
        for s in range(WIN):
            block = ext_ref[jnp.clip(start + s, 0, 3 * blocks - 1)]
            parts.append(jnp.where(s < count, block, jnp.zeros_like(block)))
        window = jnp.concatenate(parts, axis=0)
        sums = jnp.dot(ld_ref[i], window, preferred_element_type=jnp.float32)
        out_ref[i] = sums.astype(out_ref.dtype)


def impute(ext, ld_untyped, win_start, win_count, var_size):
    untyped = ld_untyped.shape[0]
    total = ext.shape[0] // BLK
    cols = ext.shape[1]
    return pl.pallas_call(
        functools.partial(impute_kernel, total // 3, var_size),
        grid_spec=pltpu.PrefetchScalarGridSpec(
            num_scalar_prefetch=2,
            grid=(untyped // UNTYPED_TILE,),
            in_specs=[
                pl.BlockSpec((total, BLK, cols), lambda i, *_: (0, 0, 0)),
                pl.BlockSpec((UNTYPED_TILE,) + ld_untyped.shape[1:], lambda i, *_: (i, 0, 0)),
            ],
            out_specs=pl.BlockSpec((UNTYPED_TILE, BLK, cols), lambda i, *_: (i, 0, 0)),
        ),
        out_shape=jax.ShapeDtypeStruct((untyped, BLK, cols), ext.dtype),
        compiler_params=pltpu.CompilerParams(vmem_limit_bytes=24 * 1024 * 1024),
        name="impute_kernel",
    )(win_start, win_count, ext.reshape(total, BLK, cols), ld_untyped)


def on_device(groups, var_size, z_typed, band_inverse, ld_untyped, trait_mix, win_start, win_count):
    ext = mixed_with_neighbours(z_typed, band_inverse, trait_mix, groups, var_size)
    imputed = impute(ext, ld_untyped, win_start, win_count, var_size)
    return imputed.reshape(ld_untyped.shape[0] * BLK, z_typed.shape[1])


def solution(mesh):
    var_size = mesh.shape["var"]
    groups = mesh.shape["sec"] * var_size
    in_specs = (
        P(("sec", "var"), "trait"),
        P(("sec", "var"), None, None),
        P(("sec", "var"), None, None),
        P(),
        P(("sec", "var")),
        P(("sec", "var")),
    )
    return jax.shard_map(
        functools.partial(on_device, groups, var_size),
        mesh=mesh, in_specs=in_specs, out_specs=P(("sec", "var"), "trait"), check_vma=False,
    )
```

```python
import functools

import jax
import jax.numpy as jnp
from jax import lax
from jax.experimental import pallas as pl
from jax.experimental.pallas import tpu as pltpu
from jax.sharding import PartitionSpec as P

BLK = 128
WIN = 4
HEAD_SIZES = (1, 1, 2, 2)
CHUNK_BLOCKS = 4
LAST_BLOCKS = 2
AHEAD = 3
UNTYPED_TILE = 8
MESH = pl.DeviceIdType.MESH


def chunk_plan(blocks):
    plan = []
    at = LAST_BLOCKS
    sizes = list(HEAD_SIZES)
    while at < blocks:
        size = min(sizes.pop(0) if sizes else CHUNK_BLOCKS, blocks - at)
        plan.append((at, size))
        at += size
    plan.append((0, LAST_BLOCKS))
    return plan


def mixed_kernel(
    plan, blocks, groups, var_size,
    z_ref, band_ref, mix_ref, ld_ref, ext_ref, ldv_ref,
    zb, bandv, w, mv, mx,
    z_sem, ld_sem, band_sem, mix_sem, own_sem, edge_send, edge_recv, xy_send, xy_recv, halo_send, halo_recv,
):
    t = lax.axis_index("trait")
    g = lax.axis_index("sec") * var_size + lax.axis_index("var")
    x_peer = t + 1 - 2 * lax.rem(t, 2)
    y_peer = t + 2 - 4 * (t // 2)
    far_peer = x_peer + y_peer - t
    x_dev, y_dev = {"trait": x_peer}, {"trait": y_peer}
    right = {"sec": (g + 1) // var_size, "var": lax.rem(g + 1, var_size)}
    left_g = lax.rem(g + groups - 1, groups)
    left = {"sec": left_g // var_size, "var": lax.rem(left_g, var_size)}
    has_left, has_right = g > 0, g < groups - 1
    rows = blocks * BLK
    order = range(len(plan))

    def rows_of(c, offset=0):
        return pl.ds(offset + plan[c][0] * BLK, plan[c][1] * BLK)

    barrier = pltpu.get_barrier_semaphore()

    def greet(device):
        pl.semaphore_signal(barrier, inc=1, device_id=device, device_id_type=MESH)

    greet(x_dev)
    greet(y_dev)
    pl.when(has_left)(lambda: greet(left))
    pl.when(has_right)(lambda: greet(right))

    def remote(src, dst, send, recv, device):
        return pltpu.make_async_remote_copy(
            src_ref=src, dst_ref=dst, send_sem=send, recv_sem=recv,
            device_id=device, device_id_type=MESH,
        )

    load_z = pltpu.make_async_copy(z_ref, zb.at[pl.ds(BLK, rows)], z_sem)
    load_z.start()
    def load_band(c):
        part = pl.ds(*plan[c])
        return pltpu.make_async_copy(band_ref.at[part], bandv.at[part], band_sem.at[c])

    for c in order:
        load_band(c).start()
    columns = pl.ds(pl.multiple_of(t * BLK, BLK), BLK)
    load_mix = [
        pltpu.make_async_copy(
            mix_ref.at[pl.ds(pl.multiple_of(peer * BLK, BLK), BLK), columns],
            mv.at[pl.ds(j * BLK, BLK)],
            mix_sem.at[j],
        )
        for j, peer in enumerate((t, x_peer, y_peer, far_peer))
    ]
    for copy in load_mix:
        copy.start()
    load_ld = pltpu.make_async_copy(ld_ref, ldv_ref, ld_sem)

    @pl.when(jnp.logical_not(has_left))
    def _():
        zb[pl.ds(0, BLK), :] = jnp.zeros((BLK, BLK), zb.dtype)

    @pl.when(jnp.logical_not(has_right))
    def _():
        zb[pl.ds(rows + BLK, BLK), :] = jnp.zeros((BLK, BLK), zb.dtype)

    edge_right = remote(
        z_ref.at[pl.ds(rows - BLK, BLK)], zb.at[pl.ds(0, BLK)], edge_send.at[0], edge_recv.at[0], right
    )
    edge_left = remote(
        z_ref.at[pl.ds(0, BLK)], zb.at[pl.ds(rows + BLK, BLK)], edge_send.at[1], edge_recv.at[1], left
    )

    def whiten(c):
        load_band(c).wait()
        if sum(plan[c]) == blocks:
            pl.when(has_right)(edge_left.wait_recv)
        if plan[c][0] == 0:
            pl.when(has_left)(edge_right.wait_recv)

        def one(i, carry):
            b = plan[c][0] + i
            first = pl.multiple_of(b * BLK, BLK)
            sums = jnp.dot(bandv[b], zb[pl.ds(first, 3 * BLK), :], preferred_element_type=jnp.float32)
            w[0, pl.ds(first, BLK), :] = sums.astype(w.dtype)
            return carry

        lax.fori_loop(0, plan[c][1], one, 0, unroll=True)

    def own_sends(c):
        part = rows_of(c)
        return (
            remote(w.at[0, part], w.at[1, part], xy_send.at[0, c], xy_recv.at[0, c], x_dev),
            remote(w.at[0, part], w.at[2, part], xy_send.at[1, c], xy_recv.at[1, c], y_dev),
        )

    def relays(c):
        first, half = plan[c][0] * BLK, plan[c][1] * BLK // 2
        lower, upper = pl.ds(first, half), pl.ds(first + half, half)
        return (
            remote(w.at[1, lower], w.at[3, lower], xy_send.at[2, c], xy_recv.at[2, c], y_dev),
            remote(w.at[2, upper], w.at[3, upper], xy_send.at[3, c], xy_recv.at[3, c], x_dev),
        )

    def halos(c):
        part = rows_of(c)
        return (
            remote(mx.at[part], ext_ref.at[part], halo_send.at[0, c], halo_recv.at[0, c], right),
            remote(
                mx.at[part], ext_ref.at[rows_of(c, 2 * rows)],
                halo_send.at[1, c], halo_recv.at[1, c], left,
            ),
        )

    def keep(c):
        return pltpu.make_async_copy(
            mx.at[rows_of(c)], ext_ref.at[rows_of(c, rows)], own_sem.at[c]
        )

    def mix(c):
        part = rows_of(c)
        all_traits = jnp.concatenate([w[j, part, :] for j in range(4)], axis=1)
        sums = jnp.dot(all_traits, mv[...], preferred_element_type=jnp.float32)
        mx[part, :] = sums.astype(mx.dtype)

    load_z.wait()
    for c in order[: AHEAD + 1]:
        whiten(c)
    pl.semaphore_wait(barrier, 2 + has_left.astype(jnp.int32) + has_right.astype(jnp.int32))
    pl.when(has_right)(edge_right.start)
    pl.when(has_left)(edge_left.start)
    for c in order[:AHEAD]:
        for copy in own_sends(c):
            copy.start()
    load_ld.start()
    for copy in load_mix:
        copy.wait()
    chunks = len(plan)
    for i in range(chunks + 1):
        if i < chunks:
            for copy in own_sends(order[i]):
                copy.wait_recv()
            for copy in relays(order[i]):
                copy.start()
            if i + AHEAD < chunks:
                for copy in own_sends(order[i + AHEAD]):
                    copy.start()
        if i >= 1:
            c = order[i - 1]
            for copy in relays(c):
                copy.wait_recv()
            mix(c)
            to_right, to_left = halos(c)
            pl.when(has_right)(to_right.start)
            pl.when(has_left)(to_left.start)
            keep(c).start()
        if i + AHEAD + 1 < chunks:
            whiten(order[i + AHEAD + 1])
    for c in order:
        for copy in own_sends(c) + relays(c):
            copy.wait_send()
        keep(c).wait()
        to_right, to_left = halos(c)

        @pl.when(has_right)
        def _():
            to_right.wait_send()
            to_left.wait_recv()

        @pl.when(has_left)
        def _():
            to_left.wait_send()
            to_right.wait_recv()

    load_ld.wait()
    pl.when(has_right)(edge_right.wait_send)
    pl.when(has_left)(edge_left.wait_send)


def mixed_with_neighbours(z_typed, band_inverse, trait_mix, ld_untyped, groups, var_size):
    rows = z_typed.shape[0]
    blocks = rows // BLK
    plan = chunk_plan(blocks)
    chunks = len(plan)
    dma = pltpu.SemaphoreType.DMA
    kind = z_typed.dtype
    return pl.pallas_call(
        functools.partial(mixed_kernel, plan, blocks, groups, var_size),
        out_shape=(pltpu.VMEM((3 * rows, BLK), kind), pltpu.VMEM(ld_untyped.shape, kind)),
        in_specs=[pl.BlockSpec(memory_space=pl.ANY)] * 4,
        out_specs=(pl.BlockSpec(memory_space=pl.ANY),) * 2,
        scratch_shapes=[
            pltpu.VMEM((rows + 2 * BLK, BLK), kind),
            pltpu.VMEM(band_inverse.shape, kind),
            pltpu.VMEM((4, rows, BLK), kind),
            pltpu.VMEM((4 * BLK, BLK), kind),
            pltpu.VMEM((rows, BLK), kind),
            dma, dma, dma((chunks,)), dma((4,)), dma((chunks,)),
            dma((2,)), dma((2,)),
            dma((4, chunks)), dma((4, chunks)),
            dma((2, chunks)), dma((2, chunks)),
        ],
        compiler_params=pltpu.CompilerParams(
            collective_id=0, has_side_effects=True, vmem_limit_bytes=16 * 1024 * 1024
        ),
        name="mixed_kernel",
    )(*(pltpu.with_memory_space_constraint(v, pltpu.HBM) for v in (z_typed, band_inverse, trait_mix, ld_untyped)))


def impute_kernel(blocks, var_size, start_ref, count_ref, ext_ref, ld_ref, out_ref):
    g = lax.axis_index("sec") * var_size + lax.axis_index("var")
    tile = out_ref.shape[0]
    first = pl.program_id(0) * tile
    for i in range(tile):
        start = start_ref[first + i] - (g - 1) * blocks
        count = count_ref[first + i]
        parts = []
        for s in range(WIN):
            block = ext_ref[jnp.clip(start + s, 0, 3 * blocks - 1)]
            parts.append(jnp.where(s < count, block, jnp.zeros_like(block)))
        window = jnp.concatenate(parts, axis=0)
        sums = jnp.dot(ld_ref[first + i], window, preferred_element_type=jnp.float32)
        out_ref[i] = sums.astype(out_ref.dtype)


def impute(ext, ld_untyped, win_start, win_count, var_size):
    untyped = ld_untyped.shape[0]
    total = ext.shape[0] // BLK
    cols = ext.shape[1]
    return pl.pallas_call(
        functools.partial(impute_kernel, total // 3, var_size),
        grid_spec=pltpu.PrefetchScalarGridSpec(
            num_scalar_prefetch=2,
            grid=(untyped // UNTYPED_TILE,),
            in_specs=[
                pl.BlockSpec(memory_space=pltpu.VMEM),
                pl.BlockSpec(memory_space=pltpu.VMEM),
            ],
            out_specs=pl.BlockSpec((UNTYPED_TILE, BLK, cols), lambda i, *_: (i, 0, 0)),
        ),
        out_shape=jax.ShapeDtypeStruct((untyped, BLK, cols), ext.dtype),
        compiler_params=pltpu.CompilerParams(vmem_limit_bytes=24 * 1024 * 1024),
        name="impute_kernel",
    )(win_start, win_count, ext.reshape(total, BLK, cols), ld_untyped)


def on_device(groups, var_size, z_typed, band_inverse, ld_untyped, trait_mix, win_start, win_count):
    ext, ld_near = mixed_with_neighbours(z_typed, band_inverse, trait_mix, ld_untyped, groups, var_size)
    imputed = impute(ext, ld_near, win_start, win_count, var_size)
    return imputed.reshape(ld_untyped.shape[0] * BLK, z_typed.shape[1])


def solution(mesh):
    var_size = mesh.shape["var"]
    groups = mesh.shape["sec"] * var_size
    in_specs = (
        P(("sec", "var"), "trait"),
        P(("sec", "var"), None, None),
        P(("sec", "var"), None, None),
        P(),
        P(("sec", "var")),
        P(("sec", "var")),
    )
    return jax.shard_map(
        functools.partial(on_device, groups, var_size),
        mesh=mesh, in_specs=in_specs, out_specs=P(("sec", "var"), "trait"), check_vma=False,
    )
```

```python
import functools

import jax
import jax.numpy as jnp
from jax import lax
from jax.experimental import pallas as pl
from jax.experimental.pallas import tpu as pltpu
from jax.sharding import PartitionSpec as P

BLK = 128
WIN = 4
HEAD_SIZES = ()
CHUNK_BLOCKS = 2
LAST_BLOCKS = 2
AHEAD = 3
LAG = 2
UNTYPED_TILE = 8
MESH = pl.DeviceIdType.MESH


def chunk_plan(blocks):
    plan = []
    at = LAST_BLOCKS
    sizes = list(HEAD_SIZES)
    while at < blocks:
        size = min(sizes.pop(0) if sizes else CHUNK_BLOCKS, blocks - at)
        plan.append((at, size))
        at += size
    plan.append((0, LAST_BLOCKS))
    return plan


def mixed_kernel(
    plan, blocks, groups, var_size,
    z_ref, band_ref, mix_ref, ld_ref, ext_ref, ldv_ref,
    zb, bandv, w, gathered, mv, results, mx,
    z_sem, ld_sem, band_sem, mix_sem, own_sem, edge_send, edge_recv, in_send, in_recv, out_send, out_recv, halo_send, halo_recv,
):
    t = lax.axis_index("trait")
    g = lax.axis_index("sec") * var_size + lax.axis_index("var")
    x_peer = t + 1 - 2 * lax.rem(t, 2)
    y_peer = t + 2 - 4 * (t // 2)
    far_peer = x_peer + y_peer - t
    peers = (t, x_peer, y_peer, far_peer)
    others = range(1, len(peers))
    right = {"sec": (g + 1) // var_size, "var": lax.rem(g + 1, var_size)}
    left_g = lax.rem(g + groups - 1, groups)
    left = {"sec": left_g // var_size, "var": lax.rem(left_g, var_size)}
    has_left, has_right = g > 0, g < groups - 1
    rows = blocks * BLK
    order = range(len(plan))

    def rows_of(c, offset=0):
        return pl.ds(offset + plan[c][0] * BLK, plan[c][1] * BLK)

    barrier = pltpu.get_barrier_semaphore()

    def greet(device):
        pl.semaphore_signal(barrier, inc=1, device_id=device, device_id_type=MESH)

    for j in others:
        greet({"trait": peers[j]})
    pl.when(has_left)(lambda: greet(left))
    pl.when(has_right)(lambda: greet(right))

    def remote(src, dst, send, recv, device):
        return pltpu.make_async_remote_copy(
            src_ref=src, dst_ref=dst, send_sem=send, recv_sem=recv,
            device_id=device, device_id_type=MESH,
        )

    load_z = pltpu.make_async_copy(z_ref, zb.at[pl.ds(BLK, rows)], z_sem)
    load_z.start()
    def load_band(c):
        part = pl.ds(*plan[c])
        return pltpu.make_async_copy(band_ref.at[part], bandv.at[part], band_sem.at[c])

    for c in order:
        load_band(c).start()
    load_mix = [
        pltpu.make_async_copy(
            mix_ref.at[
                pl.ds(pl.multiple_of(taken * BLK, BLK), BLK), pl.ds(pl.multiple_of(given * BLK, BLK), BLK)
            ],
            mv.at[pl.ds(i * BLK, BLK), pl.ds(j * BLK, BLK)],
            mix_sem.at[i, j],
        )
        for i, taken in enumerate(peers)
        for j, given in enumerate(peers)
    ]
    for copy in load_mix:
        copy.start()
    load_ld = pltpu.make_async_copy(ld_ref, ldv_ref, ld_sem)

    @pl.when(jnp.logical_not(has_left))
    def _():
        zb[pl.ds(0, BLK), :] = jnp.zeros((BLK, BLK), zb.dtype)

    @pl.when(jnp.logical_not(has_right))
    def _():
        zb[pl.ds(rows + BLK, BLK), :] = jnp.zeros((BLK, BLK), zb.dtype)

    edge_right = remote(
        z_ref.at[pl.ds(rows - BLK, BLK)], zb.at[pl.ds(0, BLK)], edge_send.at[0], edge_recv.at[0], right
    )
    edge_left = remote(
        z_ref.at[pl.ds(0, BLK)], zb.at[pl.ds(rows + BLK, BLK)], edge_send.at[1], edge_recv.at[1], left
    )

    def whiten(c):
        load_band(c).wait()
        if sum(plan[c]) == blocks:
            pl.when(has_right)(edge_left.wait_recv)
        if plan[c][0] == 0:
            pl.when(has_left)(edge_right.wait_recv)

        def one(i, carry):
            b = plan[c][0] + i
            first = pl.multiple_of(b * BLK, BLK)
            sums = jnp.dot(bandv[b], zb[pl.ds(first, 3 * BLK), :], preferred_element_type=jnp.float32)
            w[pl.ds(first, BLK), :] = sums.astype(w.dtype)
            return carry

        lax.fori_loop(0, plan[c][1], one, 0, unroll=True)

    def part_of(c, peer):
        part = plan[c][1] * BLK // len(peers)
        return pl.ds(pl.multiple_of(plan[c][0] * BLK + peer * part, part), part)

    def share_of(c):
        return pl.ds(plan[c][0] * BLK // len(peers), plan[c][1] * BLK // len(peers))

    def sends_in(c):
        return [
            remote(
                w.at[part_of(c, peers[j])], gathered.at[j - 1, share_of(c)],
                in_send.at[j - 1, c], in_recv.at[j - 1, c], {"trait": peers[j]},
            )
            for j in others
        ]

    def sends_out(c):
        return [
            remote(
                results.at[j - 1, share_of(c)], mx.at[part_of(c, t)],
                out_send.at[j - 1, c], out_recv.at[j - 1, c], {"trait": peers[j]},
            )
            for j in others
        ]

    def arrivals(c):
        return [
            remote(
                results.at[j - 1, share_of(c)], mx.at[part_of(c, peers[j])],
                out_send.at[j - 1, c], out_recv.at[j - 1, c], {"trait": peers[j]},
            )
            for j in others
        ]

    def halos(c):
        part = rows_of(c)
        return (
            remote(mx.at[part], ext_ref.at[part], halo_send.at[0, c], halo_recv.at[0, c], right),
            remote(
                mx.at[part], ext_ref.at[rows_of(c, 2 * rows)],
                halo_send.at[1, c], halo_recv.at[1, c], left,
            ),
        )

    def keep(c):
        return pltpu.make_async_copy(
            mx.at[rows_of(c)], ext_ref.at[rows_of(c, rows)], own_sem.at[c]
        )

    def mix(c):
        all_traits = jnp.concatenate(
            [w[part_of(c, t), :]] + [gathered[j - 1, share_of(c), :] for j in others], axis=1
        )
        sums = jnp.dot(all_traits, mv[...], preferred_element_type=jnp.float32).astype(mx.dtype)
        mx[part_of(c, t), :] = sums[:, :BLK]
        for j in others:
            results[j - 1, share_of(c), :] = sums[:, j * BLK : (j + 1) * BLK]

    load_z.wait()
    for c in order[: AHEAD + 1]:
        whiten(c)
    pl.semaphore_wait(barrier, len(others) + has_left.astype(jnp.int32) + has_right.astype(jnp.int32))
    pl.when(has_right)(edge_right.start)
    pl.when(has_left)(edge_left.start)
    for c in order[:AHEAD]:
        for copy in sends_in(c):
            copy.start()
    load_ld.start()
    for copy in load_mix:
        copy.wait()
    chunks = len(plan)
    for i in range(chunks + LAG):
        if i < chunks:
            for copy in sends_in(i):
                copy.wait_recv()
            mix(i)
            for copy in sends_out(i):
                copy.start()
        if i + AHEAD < chunks:
            for copy in sends_in(i + AHEAD):
                copy.start()
        if i >= LAG:
            c = i - LAG
            for copy in arrivals(c):
                copy.wait_recv()
            to_right, to_left = halos(c)
            pl.when(has_right)(to_right.start)
            pl.when(has_left)(to_left.start)
            keep(c).start()
        if i + AHEAD + 1 < chunks:
            whiten(i + AHEAD + 1)
    for c in order:
        for copy in sends_in(c) + sends_out(c):
            copy.wait_send()
        keep(c).wait()
        to_right, to_left = halos(c)

        @pl.when(has_right)
        def _():
            to_right.wait_send()
            to_left.wait_recv()

        @pl.when(has_left)
        def _():
            to_left.wait_send()
            to_right.wait_recv()

    load_ld.wait()
    pl.when(has_right)(edge_right.wait_send)
    pl.when(has_left)(edge_left.wait_send)


def mixed_with_neighbours(z_typed, band_inverse, trait_mix, ld_untyped, groups, var_size):
    rows = z_typed.shape[0]
    blocks = rows // BLK
    plan = chunk_plan(blocks)
    peers = trait_mix.shape[0] // BLK
    chunks = len(plan)
    dma = pltpu.SemaphoreType.DMA
    kind = z_typed.dtype
    return pl.pallas_call(
        functools.partial(mixed_kernel, plan, blocks, groups, var_size),
        out_shape=(pltpu.VMEM((3 * rows, BLK), kind), pltpu.VMEM(ld_untyped.shape, kind)),
        in_specs=[pl.BlockSpec(memory_space=pl.ANY)] * 4,
        out_specs=(pl.BlockSpec(memory_space=pl.ANY),) * 2,
        scratch_shapes=[
            pltpu.VMEM((rows + 2 * BLK, BLK), kind),
            pltpu.VMEM(band_inverse.shape, kind),
            pltpu.VMEM((rows, BLK), kind),
            pltpu.VMEM((peers - 1, rows // peers, BLK), kind),
            pltpu.VMEM(trait_mix.shape, kind),
            pltpu.VMEM((peers - 1, rows // peers, BLK), kind),
            pltpu.VMEM((rows, BLK), kind),
            dma, dma, dma((chunks,)), dma((peers, peers)), dma((chunks,)),
            dma((2,)), dma((2,)),
            dma((peers - 1, chunks)), dma((peers - 1, chunks)),
            dma((peers - 1, chunks)), dma((peers - 1, chunks)),
            dma((2, chunks)), dma((2, chunks)),
        ],
        compiler_params=pltpu.CompilerParams(
            collective_id=0, has_side_effects=True, vmem_limit_bytes=16 * 1024 * 1024
        ),
        name="mixed_kernel",
    )(*(pltpu.with_memory_space_constraint(v, pltpu.HBM) for v in (z_typed, band_inverse, trait_mix, ld_untyped)))


def impute_kernel(blocks, var_size, start_ref, count_ref, ext_ref, ld_ref, out_ref):
    g = lax.axis_index("sec") * var_size + lax.axis_index("var")
    tile = out_ref.shape[0]
    first = pl.program_id(0) * tile
    for i in range(tile):
        start = start_ref[first + i] - (g - 1) * blocks
        count = count_ref[first + i]
        parts = []
        for s in range(WIN):
            block = ext_ref[jnp.clip(start + s, 0, 3 * blocks - 1)]
            parts.append(jnp.where(s < count, block, jnp.zeros_like(block)))
        window = jnp.concatenate(parts, axis=0)
        sums = jnp.dot(ld_ref[first + i], window, preferred_element_type=jnp.float32)
        out_ref[i] = sums.astype(out_ref.dtype)


def impute(ext, ld_untyped, win_start, win_count, var_size):
    untyped = ld_untyped.shape[0]
    total = ext.shape[0] // BLK
    cols = ext.shape[1]
    return pl.pallas_call(
        functools.partial(impute_kernel, total // 3, var_size),
        grid_spec=pltpu.PrefetchScalarGridSpec(
            num_scalar_prefetch=2,
            grid=(untyped // UNTYPED_TILE,),
            in_specs=[
                pl.BlockSpec(memory_space=pltpu.VMEM),
                pl.BlockSpec(memory_space=pltpu.VMEM),
            ],
            out_specs=pl.BlockSpec((UNTYPED_TILE, BLK, cols), lambda i, *_: (i, 0, 0)),
        ),
        out_shape=jax.ShapeDtypeStruct((untyped, BLK, cols), ext.dtype),
        compiler_params=pltpu.CompilerParams(vmem_limit_bytes=24 * 1024 * 1024),
        name="impute_kernel",
    )(win_start, win_count, ext.reshape(total, BLK, cols), ld_untyped)


def on_device(groups, var_size, z_typed, band_inverse, ld_untyped, trait_mix, win_start, win_count):
    ext, ld_near = mixed_with_neighbours(z_typed, band_inverse, trait_mix, ld_untyped, groups, var_size)
    imputed = impute(ext, ld_near, win_start, win_count, var_size)
    return imputed.reshape(ld_untyped.shape[0] * BLK, z_typed.shape[1])


def solution(mesh):
    var_size = mesh.shape["var"]
    groups = mesh.shape["sec"] * var_size
    in_specs = (
        P(("sec", "var"), "trait"),
        P(("sec", "var"), None, None),
        P(("sec", "var"), None, None),
        P(),
        P(("sec", "var")),
        P(("sec", "var")),
    )
    return jax.shard_map(
        functools.partial(on_device, groups, var_size),
        mesh=mesh, in_specs=in_specs, out_specs=P(("sec", "var"), "trait"), check_vma=False,
    )
```

```python
import functools

import jax
import jax.numpy as jnp
from jax import lax
from jax.experimental import pallas as pl
from jax.experimental.pallas import tpu as pltpu
from jax.sharding import PartitionSpec as P

BLK = 128
WIN = 4
HEAD_SIZES = ()
CHUNK_BLOCKS = 2
LAST_BLOCKS = 2
AHEAD = 3
LAG = 2
UNTYPED_TILE = 32
MESH = pl.DeviceIdType.MESH


def chunk_plan(blocks):
    plan = []
    at = LAST_BLOCKS
    sizes = list(HEAD_SIZES)
    while at < blocks:
        size = min(sizes.pop(0) if sizes else CHUNK_BLOCKS, blocks - at)
        plan.append((at, size))
        at += size
    plan.append((0, LAST_BLOCKS))
    return plan


def mixed_kernel(
    plan, blocks, groups, var_size,
    z_ref, band_ref, mix_ref, ld_ref, ext_ref, ldv_ref,
    zb, bandv, w, gathered, mv, results, mx,
    z_sem, ld_sem, band_sem, mix_sem, own_sem, edge_send, edge_recv, in_send, in_recv, out_send, out_recv, halo_send, halo_recv,
):
    t = lax.axis_index("trait")
    g = lax.axis_index("sec") * var_size + lax.axis_index("var")
    x_peer = t + 1 - 2 * lax.rem(t, 2)
    y_peer = t + 2 - 4 * (t // 2)
    far_peer = x_peer + y_peer - t
    peers = (t, x_peer, y_peer, far_peer)
    others = range(1, len(peers))
    right = {"sec": (g + 1) // var_size, "var": lax.rem(g + 1, var_size)}
    left_g = lax.rem(g + groups - 1, groups)
    left = {"sec": left_g // var_size, "var": lax.rem(left_g, var_size)}
    has_left, has_right = g > 0, g < groups - 1
    rows = blocks * BLK
    order = range(len(plan))

    def rows_of(c, offset=0):
        return pl.ds(offset + plan[c][0] * BLK, plan[c][1] * BLK)

    barrier = pltpu.get_barrier_semaphore()

    def greet(device):
        pl.semaphore_signal(barrier, inc=1, device_id=device, device_id_type=MESH)

    for j in others:
        greet({"trait": peers[j]})
    pl.when(has_left)(lambda: greet(left))
    pl.when(has_right)(lambda: greet(right))

    def remote(src, dst, send, recv, device):
        return pltpu.make_async_remote_copy(
            src_ref=src, dst_ref=dst, send_sem=send, recv_sem=recv,
            device_id=device, device_id_type=MESH,
        )

    load_z = pltpu.make_async_copy(z_ref, zb.at[pl.ds(BLK, rows)], z_sem)
    load_z.start()
    def load_band(c):
        part = pl.ds(*plan[c])
        return pltpu.make_async_copy(band_ref.at[part], bandv.at[part], band_sem.at[c])

    for c in order:
        load_band(c).start()
    load_mix = [
        pltpu.make_async_copy(
            mix_ref.at[
                pl.ds(pl.multiple_of(taken * BLK, BLK), BLK), pl.ds(pl.multiple_of(given * BLK, BLK), BLK)
            ],
            mv.at[pl.ds(i * BLK, BLK), pl.ds(j * BLK, BLK)],
            mix_sem.at[i, j],
        )
        for i, taken in enumerate(peers)
        for j, given in enumerate(peers)
    ]
    for copy in load_mix:
        copy.start()
    load_ld = pltpu.make_async_copy(ld_ref, ldv_ref, ld_sem)

    @pl.when(jnp.logical_not(has_left))
    def _():
        zb[pl.ds(0, BLK), :] = jnp.zeros((BLK, BLK), zb.dtype)

    @pl.when(jnp.logical_not(has_right))
    def _():
        zb[pl.ds(rows + BLK, BLK), :] = jnp.zeros((BLK, BLK), zb.dtype)

    edge_right = remote(
        z_ref.at[pl.ds(rows - BLK, BLK)], zb.at[pl.ds(0, BLK)], edge_send.at[0], edge_recv.at[0], right
    )
    edge_left = remote(
        z_ref.at[pl.ds(0, BLK)], zb.at[pl.ds(rows + BLK, BLK)], edge_send.at[1], edge_recv.at[1], left
    )

    def whiten(c):
        load_band(c).wait()
        if sum(plan[c]) == blocks:
            pl.when(has_right)(edge_left.wait_recv)
        if plan[c][0] == 0:
            pl.when(has_left)(edge_right.wait_recv)

        def one(i, carry):
            b = plan[c][0] + i
            first = pl.multiple_of(b * BLK, BLK)
            sums = jnp.dot(bandv[b], zb[pl.ds(first, 3 * BLK), :], preferred_element_type=jnp.float32)
            w[pl.ds(first, BLK), :] = sums.astype(w.dtype)
            return carry

        lax.fori_loop(0, plan[c][1], one, 0, unroll=True)

    def part_of(c, peer):
        part = plan[c][1] * BLK // len(peers)
        return pl.ds(pl.multiple_of(plan[c][0] * BLK + peer * part, part), part)

    def share_of(c):
        return pl.ds(plan[c][0] * BLK // len(peers), plan[c][1] * BLK // len(peers))

    def sends_in(c):
        return [
            remote(
                w.at[part_of(c, peers[j])], gathered.at[j - 1, share_of(c)],
                in_send.at[j - 1, c], in_recv.at[j - 1, c], {"trait": peers[j]},
            )
            for j in others
        ]

    def sends_out(c):
        return [
            remote(
                results.at[j - 1, share_of(c)], mx.at[part_of(c, t)],
                out_send.at[j - 1, c], out_recv.at[j - 1, c], {"trait": peers[j]},
            )
            for j in others
        ]

    def arrivals(c):
        return [
            remote(
                results.at[j - 1, share_of(c)], mx.at[part_of(c, peers[j])],
                out_send.at[j - 1, c], out_recv.at[j - 1, c], {"trait": peers[j]},
            )
            for j in others
        ]

    def halos(c):
        part = rows_of(c)
        return (
            remote(mx.at[part], ext_ref.at[part], halo_send.at[0, c], halo_recv.at[0, c], right),
            remote(
                mx.at[part], ext_ref.at[rows_of(c, 2 * rows)],
                halo_send.at[1, c], halo_recv.at[1, c], left,
            ),
        )

    def keep(c):
        return pltpu.make_async_copy(
            mx.at[rows_of(c)], ext_ref.at[rows_of(c, rows)], own_sem.at[c]
        )

    def mix(c):
        all_traits = jnp.concatenate(
            [w[part_of(c, t), :]] + [gathered[j - 1, share_of(c), :] for j in others], axis=1
        )
        sums = jnp.dot(all_traits, mv[...], preferred_element_type=jnp.float32).astype(mx.dtype)
        mx[part_of(c, t), :] = sums[:, :BLK]
        for j in others:
            results[j - 1, share_of(c), :] = sums[:, j * BLK : (j + 1) * BLK]

    load_z.wait()
    for c in order[: AHEAD + 1]:
        whiten(c)
    pl.semaphore_wait(barrier, len(others) + has_left.astype(jnp.int32) + has_right.astype(jnp.int32))
    pl.when(has_right)(edge_right.start)
    pl.when(has_left)(edge_left.start)
    for c in order[:AHEAD]:
        for copy in sends_in(c):
            copy.start()
    load_ld.start()
    for copy in load_mix:
        copy.wait()
    chunks = len(plan)
    for i in range(chunks + LAG):
        if i < chunks:
            for copy in sends_in(i):
                copy.wait_recv()
            mix(i)
            for copy in sends_out(i):
                copy.start()
        if i + AHEAD < chunks:
            for copy in sends_in(i + AHEAD):
                copy.start()
        if i >= LAG:
            c = i - LAG
            for copy in arrivals(c):
                copy.wait_recv()
            to_right, to_left = halos(c)
            pl.when(has_right)(to_right.start)
            pl.when(has_left)(to_left.start)
            keep(c).start()
        if i + AHEAD + 1 < chunks:
            whiten(i + AHEAD + 1)
    for c in order:
        for copy in sends_in(c) + sends_out(c):
            copy.wait_send()
        keep(c).wait()
        to_right, to_left = halos(c)

        @pl.when(has_right)
        def _():
            to_right.wait_send()
            to_left.wait_recv()

        @pl.when(has_left)
        def _():
            to_left.wait_send()
            to_right.wait_recv()

    load_ld.wait()
    pl.when(has_right)(edge_right.wait_send)
    pl.when(has_left)(edge_left.wait_send)


def mixed_with_neighbours(z_typed, band_inverse, trait_mix, ld_untyped, groups, var_size):
    rows = z_typed.shape[0]
    blocks = rows // BLK
    plan = chunk_plan(blocks)
    peers = trait_mix.shape[0] // BLK
    chunks = len(plan)
    dma = pltpu.SemaphoreType.DMA
    kind = z_typed.dtype
    return pl.pallas_call(
        functools.partial(mixed_kernel, plan, blocks, groups, var_size),
        out_shape=(pltpu.VMEM((3 * rows, BLK), kind), pltpu.VMEM(ld_untyped.shape, kind)),
        in_specs=[pl.BlockSpec(memory_space=pl.ANY)] * 4,
        out_specs=(pl.BlockSpec(memory_space=pl.ANY),) * 2,
        scratch_shapes=[
            pltpu.VMEM((rows + 2 * BLK, BLK), kind),
            pltpu.VMEM(band_inverse.shape, kind),
            pltpu.VMEM((rows, BLK), kind),
            pltpu.VMEM((peers - 1, rows // peers, BLK), kind),
            pltpu.VMEM(trait_mix.shape, kind),
            pltpu.VMEM((peers - 1, rows // peers, BLK), kind),
            pltpu.VMEM((rows, BLK), kind),
            dma, dma, dma((chunks,)), dma((peers, peers)), dma((chunks,)),
            dma((2,)), dma((2,)),
            dma((peers - 1, chunks)), dma((peers - 1, chunks)),
            dma((peers - 1, chunks)), dma((peers - 1, chunks)),
            dma((2, chunks)), dma((2, chunks)),
        ],
        compiler_params=pltpu.CompilerParams(
            collective_id=0, has_side_effects=True, vmem_limit_bytes=16 * 1024 * 1024
        ),
        name="mixed_kernel",
    )(*(pltpu.with_memory_space_constraint(v, pltpu.HBM) for v in (z_typed, band_inverse, trait_mix, ld_untyped)))


def impute_kernel(blocks, var_size, start_ref, count_ref, ext_ref, ld_ref, out_ref):
    g = lax.axis_index("sec") * var_size + lax.axis_index("var")
    tile = out_ref.shape[0]
    first = pl.program_id(0) * tile
    for i in range(tile):
        start = start_ref[first + i] - (g - 1) * blocks
        count = count_ref[first + i]
        parts = []
        for s in range(WIN):
            block = ext_ref[jnp.clip(start + s, 0, 3 * blocks - 1)]
            parts.append(jnp.where(s < count, block, jnp.zeros_like(block)))
        window = jnp.concatenate(parts, axis=0)
        sums = jnp.dot(ld_ref[first + i], window, preferred_element_type=jnp.float32)
        out_ref[i] = sums.astype(out_ref.dtype)


def impute(ext, ld_untyped, win_start, win_count, var_size):
    untyped = ld_untyped.shape[0]
    total = ext.shape[0] // BLK
    cols = ext.shape[1]
    return pl.pallas_call(
        functools.partial(impute_kernel, total // 3, var_size),
        grid_spec=pltpu.PrefetchScalarGridSpec(
            num_scalar_prefetch=2,
            grid=(untyped // UNTYPED_TILE,),
            in_specs=[
                pl.BlockSpec(memory_space=pltpu.VMEM),
                pl.BlockSpec(memory_space=pltpu.VMEM),
            ],
            out_specs=pl.BlockSpec((UNTYPED_TILE, BLK, cols), lambda i, *_: (i, 0, 0)),
        ),
        out_shape=jax.ShapeDtypeStruct((untyped, BLK, cols), ext.dtype),
        compiler_params=pltpu.CompilerParams(vmem_limit_bytes=24 * 1024 * 1024),
        name="impute_kernel",
    )(win_start, win_count, ext.reshape(total, BLK, cols), ld_untyped)


def on_device(groups, var_size, z_typed, band_inverse, ld_untyped, trait_mix, win_start, win_count):
    ext, ld_near = mixed_with_neighbours(z_typed, band_inverse, trait_mix, ld_untyped, groups, var_size)
    imputed = impute(ext, ld_near, win_start, win_count, var_size)
    return imputed.reshape(ld_untyped.shape[0] * BLK, z_typed.shape[1])


def solution(mesh):
    var_size = mesh.shape["var"]
    groups = mesh.shape["sec"] * var_size
    in_specs = (
        P(("sec", "var"), "trait"),
        P(("sec", "var"), None, None),
        P(("sec", "var"), None, None),
        P(),
        P(("sec", "var")),
        P(("sec", "var")),
    )
    return jax.shard_map(
        functools.partial(on_device, groups, var_size),
        mesh=mesh, in_specs=in_specs, out_specs=P(("sec", "var"), "trait"), check_vma=False,
    )
```

```python
import functools

import jax
import jax.numpy as jnp
from jax import lax
from jax.experimental import pallas as pl
from jax.experimental.pallas import tpu as pltpu
from jax.sharding import PartitionSpec as P

BLK = 128
WIN = 4
HEAD_SIZES = ()
CHUNK_BLOCKS = 4
LAST_BLOCKS = 2
AHEAD = 2
LAG = 1
UNTYPED_TILE = 32
MESH = pl.DeviceIdType.MESH


def chunk_plan(blocks):
    plan = []
    at = LAST_BLOCKS
    sizes = list(HEAD_SIZES)
    while at < blocks:
        size = min(sizes.pop(0) if sizes else CHUNK_BLOCKS, blocks - at)
        plan.append((at, size))
        at += size
    plan.append((0, LAST_BLOCKS))
    return plan


def mixed_kernel(
    plan, blocks, groups, var_size,
    z_ref, band_ref, mix_ref, ld_ref, ext_ref, ldv_ref,
    zb, bandv, w, gathered, mv, results, mx,
    z_sem, ld_sem, band_sem, mix_sem, own_sem, edge_send, edge_recv, in_send, in_recv, out_send, out_recv, halo_send, halo_recv,
):
    t = lax.axis_index("trait")
    g = lax.axis_index("sec") * var_size + lax.axis_index("var")
    x_peer = t + 1 - 2 * lax.rem(t, 2)
    y_peer = t + 2 - 4 * (t // 2)
    far_peer = x_peer + y_peer - t
    peers = (t, x_peer, y_peer, far_peer)
    others = range(1, len(peers))
    right = {"sec": (g + 1) // var_size, "var": lax.rem(g + 1, var_size)}
    left_g = lax.rem(g + groups - 1, groups)
    left = {"sec": left_g // var_size, "var": lax.rem(left_g, var_size)}
    has_left, has_right = g > 0, g < groups - 1
    rows = blocks * BLK
    order = range(len(plan))

    def rows_of(c, offset=0):
        return pl.ds(offset + plan[c][0] * BLK, plan[c][1] * BLK)

    barrier = pltpu.get_barrier_semaphore()

    def greet(device):
        pl.semaphore_signal(barrier, inc=1, device_id=device, device_id_type=MESH)

    for j in others:
        greet({"trait": peers[j]})
    pl.when(has_left)(lambda: greet(left))
    pl.when(has_right)(lambda: greet(right))

    def remote(src, dst, send, recv, device):
        return pltpu.make_async_remote_copy(
            src_ref=src, dst_ref=dst, send_sem=send, recv_sem=recv,
            device_id=device, device_id_type=MESH,
        )

    load_z = pltpu.make_async_copy(z_ref, zb.at[pl.ds(BLK, rows)], z_sem)
    load_z.start()
    def load_band(c):
        part = pl.ds(*plan[c])
        return pltpu.make_async_copy(band_ref.at[part], bandv.at[part], band_sem.at[c])

    for c in order:
        load_band(c).start()
    load_mix = [
        pltpu.make_async_copy(
            mix_ref.at[
                pl.ds(pl.multiple_of(taken * BLK, BLK), BLK), pl.ds(pl.multiple_of(given * BLK, BLK), BLK)
            ],
            mv.at[pl.ds(i * BLK, BLK), pl.ds(j * BLK, BLK)],
            mix_sem.at[i, j],
        )
        for i, taken in enumerate(peers)
        for j, given in enumerate(peers)
    ]
    for copy in load_mix:
        copy.start()
    load_ld = pltpu.make_async_copy(ld_ref, ldv_ref, ld_sem)

    @pl.when(jnp.logical_not(has_left))
    def _():
        zb[pl.ds(0, BLK), :] = jnp.zeros((BLK, BLK), zb.dtype)

    @pl.when(jnp.logical_not(has_right))
    def _():
        zb[pl.ds(rows + BLK, BLK), :] = jnp.zeros((BLK, BLK), zb.dtype)

    edge_right = remote(
        z_ref.at[pl.ds(rows - BLK, BLK)], zb.at[pl.ds(0, BLK)], edge_send.at[0], edge_recv.at[0], right
    )
    edge_left = remote(
        z_ref.at[pl.ds(0, BLK)], zb.at[pl.ds(rows + BLK, BLK)], edge_send.at[1], edge_recv.at[1], left
    )

    def whiten(c):
        load_band(c).wait()
        if sum(plan[c]) == blocks:
            pl.when(has_right)(edge_left.wait_recv)
        if plan[c][0] == 0:
            pl.when(has_left)(edge_right.wait_recv)

        def one(i, carry):
            b = plan[c][0] + i
            first = pl.multiple_of(b * BLK, BLK)
            sums = jnp.dot(bandv[b], zb[pl.ds(first, 3 * BLK), :], preferred_element_type=jnp.float32)
            w[pl.ds(first, BLK), :] = sums.astype(w.dtype)
            return carry

        lax.fori_loop(0, plan[c][1], one, 0, unroll=True)

    def part_of(c, peer):
        part = plan[c][1] * BLK // len(peers)
        return pl.ds(pl.multiple_of(plan[c][0] * BLK + peer * part, part), part)

    def share_of(c):
        return pl.ds(plan[c][0] * BLK // len(peers), plan[c][1] * BLK // len(peers))

    def sends_in(c):
        return [
            remote(
                w.at[part_of(c, peers[j])], gathered.at[j - 1, share_of(c)],
                in_send.at[j - 1, c], in_recv.at[j - 1, c], {"trait": peers[j]},
            )
            for j in others
        ]

    def sends_out(c):
        return [
            remote(
                results.at[j - 1, share_of(c)], mx.at[part_of(c, t)],
                out_send.at[j - 1, c], out_recv.at[j - 1, c], {"trait": peers[j]},
            )
            for j in others
        ]

    def arrivals(c):
        return [
            remote(
                results.at[j - 1, share_of(c)], mx.at[part_of(c, peers[j])],
                out_send.at[j - 1, c], out_recv.at[j - 1, c], {"trait": peers[j]},
            )
            for j in others
        ]

    def halos(c, j):
        part = plan[c][1] * BLK // len(peers)
        above = pl.ds(pl.multiple_of(2 * rows + plan[c][0] * BLK + peers[j] * part, part), part)
        mine = part_of(c, peers[j])
        return (
            remote(mx.at[mine], ext_ref.at[mine], halo_send.at[0, j, c], halo_recv.at[0, j, c], right),
            remote(mx.at[mine], ext_ref.at[above], halo_send.at[1, j, c], halo_recv.at[1, j, c], left),
        )

    def send_halos(c, j):
        to_right, to_left = halos(c, j)
        pl.when(has_right)(to_right.start)
        pl.when(has_left)(to_left.start)

    def keep(c):
        return pltpu.make_async_copy(
            mx.at[rows_of(c)], ext_ref.at[rows_of(c, rows)], own_sem.at[c]
        )

    def mix(c):
        all_traits = jnp.concatenate(
            [w[part_of(c, t), :]] + [gathered[j - 1, share_of(c), :] for j in others], axis=1
        )
        sums = jnp.dot(all_traits, mv[...], preferred_element_type=jnp.float32).astype(mx.dtype)
        mx[part_of(c, t), :] = sums[:, :BLK]
        for j in others:
            results[j - 1, share_of(c), :] = sums[:, j * BLK : (j + 1) * BLK]

    load_z.wait()
    for c in order[: AHEAD + 1]:
        whiten(c)
    pl.semaphore_wait(barrier, len(others) + has_left.astype(jnp.int32) + has_right.astype(jnp.int32))
    pl.when(has_right)(edge_right.start)
    pl.when(has_left)(edge_left.start)
    for c in order[:AHEAD]:
        for copy in sends_in(c):
            copy.start()
    load_ld.start()
    for copy in load_mix:
        copy.wait()
    chunks = len(plan)
    for i in range(chunks + LAG):
        if i < chunks:
            for copy in sends_in(i):
                copy.wait_recv()
            mix(i)
            for copy in sends_out(i):
                copy.start()
            send_halos(i, 0)
        if i + AHEAD < chunks:
            for copy in sends_in(i + AHEAD):
                copy.start()
        if i >= LAG:
            c = i - LAG
            for j, copy in zip(others, arrivals(c)):
                copy.wait_recv()
                send_halos(c, j)
            keep(c).start()
        if i + AHEAD + 1 < chunks:
            whiten(i + AHEAD + 1)
    for c in order:
        for copy in sends_in(c) + sends_out(c):
            copy.wait_send()
        keep(c).wait()
        every = [halos(c, j) for j in range(len(peers))]

        @pl.when(has_right)
        def _():
            for to_right, to_left in every:
                to_right.wait_send()
                to_left.wait_recv()

        @pl.when(has_left)
        def _():
            for to_right, to_left in every:
                to_left.wait_send()
                to_right.wait_recv()

    load_ld.wait()
    pl.when(has_right)(edge_right.wait_send)
    pl.when(has_left)(edge_left.wait_send)


def mixed_with_neighbours(z_typed, band_inverse, trait_mix, ld_untyped, groups, var_size):
    rows = z_typed.shape[0]
    blocks = rows // BLK
    plan = chunk_plan(blocks)
    peers = trait_mix.shape[0] // BLK
    chunks = len(plan)
    dma = pltpu.SemaphoreType.DMA
    kind = z_typed.dtype
    return pl.pallas_call(
        functools.partial(mixed_kernel, plan, blocks, groups, var_size),
        out_shape=(pltpu.VMEM((3 * rows, BLK), kind), pltpu.VMEM(ld_untyped.shape, kind)),
        in_specs=[pl.BlockSpec(memory_space=pl.ANY)] * 4,
        out_specs=(pl.BlockSpec(memory_space=pl.ANY),) * 2,
        scratch_shapes=[
            pltpu.VMEM((rows + 2 * BLK, BLK), kind),
            pltpu.VMEM(band_inverse.shape, kind),
            pltpu.VMEM((rows, BLK), kind),
            pltpu.VMEM((peers - 1, rows // peers, BLK), kind),
            pltpu.VMEM(trait_mix.shape, kind),
            pltpu.VMEM((peers - 1, rows // peers, BLK), kind),
            pltpu.VMEM((rows, BLK), kind),
            dma, dma, dma((chunks,)), dma((peers, peers)), dma((chunks,)),
            dma((2,)), dma((2,)),
            dma((peers - 1, chunks)), dma((peers - 1, chunks)),
            dma((peers - 1, chunks)), dma((peers - 1, chunks)),
            dma((2, peers, chunks)), dma((2, peers, chunks)),
        ],
        compiler_params=pltpu.CompilerParams(
            collective_id=0, has_side_effects=True, vmem_limit_bytes=16 * 1024 * 1024
        ),
        name="mixed_kernel",
    )(*(pltpu.with_memory_space_constraint(v, pltpu.HBM) for v in (z_typed, band_inverse, trait_mix, ld_untyped)))


def impute_kernel(blocks, var_size, start_ref, count_ref, ext_ref, ld_ref, out_ref):
    g = lax.axis_index("sec") * var_size + lax.axis_index("var")
    tile = out_ref.shape[0]
    first = pl.program_id(0) * tile
    for i in range(tile):
        start = start_ref[first + i] - (g - 1) * blocks
        count = count_ref[first + i]
        parts = []
        for s in range(WIN):
            block = ext_ref[jnp.clip(start + s, 0, 3 * blocks - 1)]
            parts.append(jnp.where(s < count, block, jnp.zeros_like(block)))
        window = jnp.concatenate(parts, axis=0)
        sums = jnp.dot(ld_ref[first + i], window, preferred_element_type=jnp.float32)
        out_ref[i] = sums.astype(out_ref.dtype)


def impute(ext, ld_untyped, win_start, win_count, var_size):
    untyped = ld_untyped.shape[0]
    total = ext.shape[0] // BLK
    cols = ext.shape[1]
    return pl.pallas_call(
        functools.partial(impute_kernel, total // 3, var_size),
        grid_spec=pltpu.PrefetchScalarGridSpec(
            num_scalar_prefetch=2,
            grid=(untyped // UNTYPED_TILE,),
            in_specs=[
                pl.BlockSpec(memory_space=pltpu.VMEM),
                pl.BlockSpec(memory_space=pltpu.VMEM),
            ],
            out_specs=pl.BlockSpec((UNTYPED_TILE, BLK, cols), lambda i, *_: (i, 0, 0)),
        ),
        out_shape=jax.ShapeDtypeStruct((untyped, BLK, cols), ext.dtype),
        compiler_params=pltpu.CompilerParams(vmem_limit_bytes=24 * 1024 * 1024),
        name="impute_kernel",
    )(win_start, win_count, ext.reshape(total, BLK, cols), ld_untyped)


def on_device(groups, var_size, z_typed, band_inverse, ld_untyped, trait_mix, win_start, win_count):
    ext, ld_near = mixed_with_neighbours(z_typed, band_inverse, trait_mix, ld_untyped, groups, var_size)
    imputed = impute(ext, ld_near, win_start, win_count, var_size)
    return imputed.reshape(ld_untyped.shape[0] * BLK, z_typed.shape[1])


def solution(mesh):
    var_size = mesh.shape["var"]
    groups = mesh.shape["sec"] * var_size
    in_specs = (
        P(("sec", "var"), "trait"),
        P(("sec", "var"), None, None),
        P(("sec", "var"), None, None),
        P(),
        P(("sec", "var")),
        P(("sec", "var")),
    )
    return jax.shard_map(
        functools.partial(on_device, groups, var_size),
        mesh=mesh, in_specs=in_specs, out_specs=P(("sec", "var"), "trait"), check_vma=False,
    )
```
